256 devices in a mesh: depth: 128 (over y, x, z_lo, core), src: 2 (over z_hi).
Axes of the slice: x: 4, y: 4, z: 8 (z_hi: 2, z_lo: 4; z = z_hi * 4 + z_lo), core: 2. Of those that a mesh axis runs over, the one named last changes fastest.
Arguments:
- angles: int32 [4], P('src'), may hold values from 0 to 63
- factor_choice: int32 [256], P('depth'), may hold values from 0 to 1
- contrast: float32 [256, 256], P('depth'), may hold values from -1 to 1
- adjoint_source: float32 [2, 4, 256, 256], P(None, 'src', 'depth'), may hold values from -1 to 1
- inverse_blocks: float32 [256, 2, 2, 128, 128], P('depth')
Outputs:
- gradient: float32 [256, 256], P('depth', 'src')
The draws below stay inside these ranges and needn't reach their ends.
All inputs are finite; a program needn't handle non-finite values.
Results may differ from the reference program's by a relative error of at most 0.0003.
Values sent between devices are 32-bit elements; how exact they have to be, the bound alone decides.
No kernel may reach another device: no remote copies, remote signals or barrier semaphores. Data moves between devices by JAX's collectives and lax.ppermute only.
A program may use at most 192 MiB of HBM per device.

```python
import math
import jax
import jax.numpy as jnp
from jax import lax

B = 128
TILES = 2
ZD = 2
BANK = 2
NANG = 64
LAYERS = 256
LAYER_MULTIPLIER = 256
SOURCES = 4
CELLS = 256


def draw_inverse_blocks(key, part):
    stochastic_seeds = jax.random.split(key, 5)
    fast_share = 0.25
    faster_choice_indicator = jax.random.uniform(stochastic_seeds[0], (TILES, B)) < fast_share
    slower_portion_count = math.sqrt(1.0 - 0.04 - 0.5 / LAYERS)
    faster_portion_count = jax.random.uniform(stochastic_seeds[1], (LAYER_MULTIPLIER, TILES, B), minval=0.4, maxval=0.85)
    heavy_choice_indicator = jax.random.uniform(stochastic_seeds[2], (LAYER_MULTIPLIER, 1, 1)) < 1.0 / 32.0
    wavefield_amplitude = jnp.where(faster_choice_indicator[None], faster_portion_count, slower_portion_count) * jnp.where(heavy_choice_indicator, 0.7, 1.0)
    angle_part = jax.random.uniform(stochastic_seeds[3], (LAYER_MULTIPLIER, TILES, B), minval=-math.pi, maxval=math.pi)
    noise_part = jax.random.normal(stochastic_seeds[4], (LAYER_MULTIPLIER, TILES, 2, B, B)) * (0.2 * math.sqrt(0.5) / math.sqrt(B))
    identity = jnp.eye(B, dtype=jnp.float32)
    diagonal = jnp.stack([wavefield_amplitude * jnp.cos(angle_part), wavefield_amplitude * jnp.sin(angle_part)], axis=2)
    return (diagonal[..., None] * identity + noise_part * (1.0 - identity)).astype(jnp.float32)


def with_ends(array, stream_key, least, high):
    dims = array.shape
    place = [jax.random.randint(jax.random.fold_in(stream_key, axis), (), 0, dims[axis]) for axis in range(len(dims))]
    array = array.at[tuple(place)].set(least)
    longest = dims.index(max(dims))
    place[longest] = (place[longest] + 1) % dims[longest]
    return array.at[tuple(place)].set(high)


def level_of(key, dims, shards, low, largest):
    def one(axis_at, shards_of):
        heights = jax.random.uniform(jax.random.fold_in(jax.random.fold_in(key, 6), axis_at), (shards_of,), jnp.float32, low / len(shards), largest / len(shards))
        return jnp.repeat(jnp.exp(heights), dims[axis_at] // shards_of).reshape((-1,) + (1,) * (len(dims) - axis_at - 1))

    factor_of = one(*shards[0])
    for cut in shards[1:]:
        factor_of = factor_of * one(*cut)
    return factor_of


def noise(rng, extent, width, most, shards=(), held_as=jnp.bfloat16):
    result = width * jax.random.normal(rng, extent, jnp.float32)
    if shards:
        result = result * level_of(rng, extent, shards, -0.22, 0.18)
    return jnp.clip(result, -most, most).astype(held_as)


def setup_inputs(seed: int = 0) -> dict:
    arg_keys = jax.random.split(jax.random.key(seed), 6)
    return {
        "angles": with_ends(jax.random.randint(arg_keys[0], (SOURCES,), 0, NANG), jax.random.fold_in(arg_keys[0], 1), 0, NANG - 1).astype(jnp.int32),
        "factor_choice": with_ends(jax.random.randint(arg_keys[1], (LAYERS,), 0, BANK), jax.random.fold_in(arg_keys[1], 1), 0, BANK - 1).astype(jnp.int32),
        "contrast": noise(arg_keys[2], (LAYERS, CELLS), 0.15, 1.0, ((0, 128),), jnp.float32),
        "adjoint_source": noise(arg_keys[3], (2, SOURCES, LAYERS, CELLS), 0.15, 1.0, ((1, 2), (2, 128)), jnp.float32),
        "inverse_blocks": draw_inverse_blocks(jax.random.fold_in(arg_keys[5], 71), 0),
    }


PRECISE = lax.Precision.HIGHEST
WAVENUMBER = 0.8


def apply_block(factor, carried):
    real_part = jnp.einsum("tij,ftj->fti", factor[:, 0], carried[0], precision=PRECISE) - jnp.einsum("tij,ftj->fti", factor[:, 1], carried[1], precision=PRECISE)
    imag_part = jnp.einsum("tij,ftj->fti", factor[:, 0], carried[1], precision=PRECISE) + jnp.einsum("tij,ftj->fti", factor[:, 1], carried[0], precision=PRECISE)
    return jnp.stack([real_part, imag_part])


def incident_wave(angles, layers, first_layer, lateral_cells):
    direction = angles.astype(jnp.float32) * (2.0 * math.pi / NANG)
    depth_pos = first_layer + jnp.arange(layers).astype(jnp.float32)
    lateral = (jnp.arange(lateral_cells) % B).astype(jnp.float32)
    phase_arg = WAVENUMBER * (jnp.sin(direction)[:, None, None] * lateral[None, None, :] + jnp.cos(direction)[:, None, None] * depth_pos[None, :, None])
    return jnp.stack([jnp.cos(phase_arg), jnp.sin(phase_arg)])


def reference(angles, factor_choice, contrast, adjoint_source, inverse_blocks):
    sources = angles.shape[0]
    layers, lateral_cells = contrast.shape
    tile_count = lateral_cells // B
    incident = incident_wave(angles, layers, 0.0, lateral_cells)
    forcing = incident * contrast[None, None]
    fields = jnp.concatenate([forcing, adjoint_source], axis=1)
    fields = fields.reshape(2, 2 * sources, layers, tile_count, B).transpose(2, 0, 1, 3, 4)
    slots = ((jnp.arange(layers) // ZD) * BANK + factor_choice).astype(jnp.int32)

    def down_step(carried, element):
        force, slot_index = element
        updated = apply_block(inverse_blocks[slot_index], force + carried)
        return updated, updated

    zero_state = jnp.zeros(fields.shape[1:], jnp.float32)
    _, downward = lax.scan(down_step, zero_state, (fields, slots))

    def up_step(carried, element):
        previous, slot_index = element
        updated = previous + apply_block(inverse_blocks[slot_index], carried)
        return updated, updated

    _, upward = lax.scan(up_step, zero_state, (downward, slots), reverse=True)
    solved = upward.transpose(1, 2, 0, 3, 4).reshape(2, 2 * sources, layers, lateral_cells)
    total_field = incident + solved[:, :sources]
    adjoint = solved[:, sources:]
    return jnp.sum(total_field[0] * adjoint[0] - total_field[1] * adjoint[1], axis=0) / sources
```

```python
import functools
import math

import jax
import jax.numpy as jnp
from jax import lax
from jax.experimental import pallas as pl
from jax.experimental.pallas import tpu as pltpu
from jax.sharding import PartitionSpec as P

B = 128
W2 = 2 * B
NANG = 64
WAVENUMBER = 0.8
FIELDS = 8
ROWS = B + FIELDS
F32 = jnp.float32
BF16 = jnp.bfloat16


def split(v):
    hi = v.astype(BF16)
    return hi, (v - hi.astype(F32)).astype(BF16)


def wide(part):
    re, im = part[:, :B], part[:, B:]
    return jnp.concatenate([part, jnp.concatenate([-im, re], axis=1)], axis=0)


def weights(t):
    hi, lo = split(t)
    return wide(hi), wide(lo)


def dot(a, b):
    return jnp.dot(a, b, preferred_element_type=F32)


def mul(v, w):
    hi, lo = split(v)
    return (dot(lo, w[0]) + dot(hi, w[1])) + dot(hi, w[0])


def mulv(v, w):
    n = v.shape[0]
    hi, lo = split(v)
    both = jnp.concatenate([hi, lo], axis=0)
    a, b = dot(both, w[0]), dot(both, w[1])
    return (a[n:] + b[:n]) + a[:n]


def coords():
    d = lax.axis_index("depth")
    return d & 1, (d >> 1) & 3, (d >> 3) & 3, (d >> 5) & 3


def place(shift):
    d = lax.axis_index("depth")
    core = d & 1
    at = (d >> shift) & 3
    return jnp.where(core == 0, at, 3 - at)


def prep_kernel(angles, choice, contrast, adj, blocks, own, oth, raw, sem):
    t = lax.axis_index("src")
    first = (lax.axis_index("depth") * 2).astype(F32)
    copies = [
        pltpu.make_async_copy(blocks.at[choice[l], t], raw.at[l], sem.at[l]) for l in range(2)
    ]
    for c in copies:
        c.start()
    row = lax.broadcasted_iota(jnp.int32, (FIELDS, B), 0)
    lane = lax.broadcasted_iota(jnp.int32, (FIELDS, B), 1).astype(F32)
    odd = (row & 1) == 1
    unit = 2.0 * math.pi / NANG
    direction = (
        jnp.where(odd, jnp.full((FIELDS, B), angles[1]), jnp.full((FIELDS, B), angles[0])).astype(F32)
        * unit
    )
    sn, cs = jnp.sin(direction), jnp.cos(direction)
    zero = jnp.zeros((FIELDS, B), F32)
    for l in range(2):
        arg = WAVENUMBER * (sn * lane + cs * (first + float(l)))
        inc = (jnp.cos(arg), jnp.sin(arg))
        for out, tile, shift, top in ((own, t, 0, B), (oth, 1 - t, 2, 0)):
            is_f = (row >= shift) & (row < shift + 2)
            is_a = (row >= shift + 4) & (row < shift + 6)

            def tiled(line):
                return jnp.where(tile == 0, line[:, :B], line[:, B:])

            con = tiled(contrast[pl.ds(l, 1), :])
            for p in range(2):
                a = jnp.where(odd, tiled(adj[p, 1, pl.ds(l, 1), :]), tiled(adj[p, 0, pl.ds(l, 1), :]))
                part = slice(p * B, (p + 1) * B)
                out[l, top : top + 8, part] = jnp.where(is_f, inc[p] * con, jnp.where(is_a, a, zero))
                out[l, top + 8 : top + 16, part] = jnp.where(is_f, inc[p], zero)
    for l in range(2):
        copies[l].wait()
        own[l, :B, :B] = raw[l, 0].T
        own[l, :B, B:] = raw[l, 1].T


def chip_kernel(own, peer, x):
    core = lax.axis_index("depth") & 1
    g = [(own if s < 2 else peer)[(s & 1) ^ core, :B, :] for s in range(4)]
    x01 = mul(g[0], weights(g[1]))
    x23 = mul(g[2], weights(g[3]))
    x[...] = mul(x01, weights(x23))


def offset_kernel(own, peer, same, cross, xm, x):
    core = lax.axis_index("depth") & 1
    x[:B, :] = xm[...]
    v = jnp.zeros((FIELDS, W2), F32)
    for k in range(4):
        a, b = (own, same) if k < 2 else (peer, cross)
        h = a[k & 1, B : B + 8, :] + b[k & 1, :8, :]
        v = mulv(v + h, weights(a[k & 1, :B, :]))
    x[B:, :] = jnp.where(core == 0, v, 0.0)


def level_kernel(shift, r0, r1, r2, r3, x, s, p, v):
    q = place(shift)
    for k, r in enumerate((r0, r1, r2, r3)):
        s[q ^ k] = r[...]
    row = lax.broadcasted_iota(jnp.int32, (ROWS, W2), 0)
    col = lax.broadcasted_iota(jnp.int32, (ROWS, W2), 1)
    tail = row >= B

    def step(a, b):
        return mul(a, weights(b[:B])) + jnp.where(tail, b, 0.0)

    s0, s1, s2, s3 = (s[k] for k in range(4))
    x01 = step(s0, s1)
    x23 = step(s2, s3)
    x[...] = step(x01, x23)
    x012 = step(x01, s2)
    one = jnp.where((row == col) & (row < B), 1.0, 0.0)
    p[...] = jnp.where(q == 0, one, jnp.where(q == 1, s0, jnp.where(q == 2, x01, x012)))
    v[0] = x23[:B]
    v[1] = mul(s1[:B], weights(x23[:B]))


def turn_kernel(r0, r1, r2, r3, pz, px, own, peer, same, cross, out, s):
    q = place(5)
    for k, r in enumerate((r0, r1, r2, r3)):
        s[q ^ k] = r[...]
    a = jnp.where(q > 0, s[0, B:, :], 0.0)
    for k in (1, 2):
        a = jnp.where(q > k, mulv(a, weights(s[k, :B, :])) + s[k, B:, :], a)
    for p in (px, pz):
        a = mulv(a, weights(p[:B, :])) + p[B:, :]
    ws, ds = [], []
    for k in range(4):
        g, o = (own, same) if k < 2 else (peer, cross)
        w = weights(g[k & 1, :B, :])
        a = mulv(a + (g[k & 1, B : B + 8, :] + o[k & 1, :8, :]), w)
        ws.append(w)
        ds.append(a)
        out[8 + 8 * k : 16 + 8 * k, :] = a
    u = ds[3]
    for k in (2, 1, 0):
        u = ds[k] + mulv(u, ws[k])
    out[:8, :] = u


def gather_kernel(shift, r0, r1, r2, r3, s, v, total, part, e):
    q = place(shift)
    for k, r in enumerate((r0, r1, r2, r3)):
        e[q ^ k] = r[...]
    total[...] = (
        (mulv(e[0], weights(v[1])) + mulv(e[1], weights(v[0])))
        + mulv(e[2], weights(s[3, :B, :]))
        + e[3]
    )
    c = jnp.where(q > 0, e[0], 0.0)
    for k in (1, 2):
        c = jnp.where(q > k, mulv(c, weights(s[k, :B, :])) + e[k], c)
    part[...] = c


def last_kernel(e0, e1, e2, e3, r0, r1, r2, r3, px, pz, cx, cz, own, peer, same, cross, d, grad, e, s):
    q = place(5)
    for k, (f, r) in enumerate(((e0, r0), (e1, r1), (e2, r2), (e3, r3))):
        e[q ^ k] = f[...]
        s[q ^ k] = r[...]
    u = jnp.where(q > 0, e[0], 0.0)
    for k in (1, 2):
        u = jnp.where(q > k, mulv(u, weights(s[k, :B, :])) + e[k], u)
    for p, c in ((px, cx), (pz, cz)):
        u = mulv(u, weights(p[:B, :])) + c[...]
    for k in (3, 2, 1, 0):
        g, o = (peer, cross) if k < 2 else (own, same)
        u = d[8 + 8 * k : 16 + 8 * k, :] + mulv(u, weights(g[k & 1, :B, :]))
        f = u + (g[k & 1, B + 8 : B + 16, :] + o[k & 1, 8:16, :])
        prod = f[:4] * f[4:]
        tot = jnp.sum(prod, axis=0, keepdims=True)
        grad[k : k + 1, :] = (tot[:, :B] - tot[:, B:]) * 0.25


def call(kernel, outs, *args, scratch=(), in_specs=None, name=None):
    shapes = [jax.ShapeDtypeStruct(o, F32) for o in outs]
    vm = pl.BlockSpec(memory_space=pltpu.VMEM)
    got = pl.pallas_call(
        kernel,
        out_shape=shapes,
        in_specs=in_specs or [vm] * len(args),
        out_specs=[vm] * len(outs),
        scratch_shapes=list(scratch),
        cost_estimate=pl.CostEstimate(flops=200_000_000, bytes_accessed=1_000_000, transcendentals=0),
        name=name,
    )(*args)
    return got[0] if len(outs) == 1 else got


def gather4(value, bit, depth, odd_only=False):
    pick = [i for i in range(depth) if not odd_only or i & 1]
    return [value] + [
        lax.ppermute(value, "depth", [(i, i ^ (k * bit)) for i in pick]) for k in (1, 2, 3)
    ]


def per_device(angles, factor_choice, contrast, adjoint_source, inverse_blocks):
    depth = lax.axis_size("depth")
    core = lax.axis_index("depth") & 1
    vm = pl.BlockSpec(memory_space=pltpu.VMEM)
    sm = pl.BlockSpec(memory_space=pltpu.SMEM)
    own, oth = call(
        prep_kernel,
        [(2, B + 16, W2), (2, 16, W2)],
        angles, factor_choice, contrast, adjoint_source, inverse_blocks,
        in_specs=[sm, sm, vm, vm, pl.BlockSpec(memory_space=pl.ANY)],
        scratch=[pltpu.VMEM((2, 2, B, B), F32), pltpu.SemaphoreType.DMA((2,))],
        name="prep",
    )
    swap = [(i, i ^ 1) for i in range(depth)]
    peer = lax.ppermute(own, "depth", swap)
    same = lax.ppermute(oth, "src", [(0, 1), (1, 0)])
    cross = lax.ppermute(
        oth, ("depth", "src"), [(2 * i + t, 2 * (i ^ 1) + (1 - t)) for i in range(depth) for t in range(2)]
    )
    xm = call(chip_kernel, [(B, W2)], own, peer, name="chip")
    x = call(offset_kernel, [(ROWS, W2)], own, peer, same, cross, xm, name="offset")
    outs = [(ROWS, W2), (4, ROWS, W2), (ROWS, W2), (2, B, W2)]
    x, sz, pz, vz = call(functools.partial(level_kernel, 1), outs, *gather4(x, 2, depth), name="level_z")
    x, sx, px, vx = call(functools.partial(level_kernel, 3), outs, *gather4(x, 8, depth), name="level_x")
    ry = gather4(x, 32, depth)
    big = pltpu.VMEM((4, ROWS, W2), F32)
    small = pltpu.VMEM((4, FIELDS, W2), F32)
    sent = call(
        turn_kernel, [(40, W2)], *ry, pz, px, own, peer, same, cross, scratch=[big], name="turn"
    )
    d = lax.ppermute(sent, "depth", [(i, i + 1) for i in range(0, depth, 2)])
    two = [(FIELDS, W2), (FIELDS, W2)]
    ez = gather4(d[:FIELDS], 2, depth, True)
    e, cz = call(functools.partial(gather_kernel, 1), two, *ez, sz, vz, scratch=[small], name="up_z")
    ex = gather4(e, 8, depth, True)
    e, cx = call(functools.partial(gather_kernel, 3), two, *ex, sx, vx, scratch=[small], name="up_x")
    ey = gather4(e, 32, depth, True)
    grad = call(
        last_kernel, [(4, B)], *ey, *ry, px, pz, cx, cz, own, peer, same, cross, d,
        scratch=[small, big], name="last",
    )
    back = lax.ppermute(grad[:2], "depth", [(i + 1, i) for i in range(0, depth, 2)])
    return jnp.where(core == 0, back, grad[2:])


def solution(mesh):
    placed = (
        P("src"),
        P("depth"),
        P("depth", None),
        P(None, "src", "depth", None),
        P("depth", None, None, None, None),
    )
    return jax.shard_map(
        per_device, mesh=mesh, in_specs=placed, out_specs=P("depth", "src"), check_vma=False
    )
```

```python
import functools
import math

import jax
import jax.numpy as jnp
from jax import lax
from jax.experimental import pallas as pl
from jax.experimental.pallas import tpu as pltpu
from jax.sharding import PartitionSpec as P


B = 128
W2 = 2 * B
NANG = 64
WAVENUMBER = 0.8
FIELDS = 8
ROWS = B + FIELDS
F32 = jnp.float32
BF16 = jnp.bfloat16


def split(v):
    hi = v.astype(BF16)
    return hi, (v - hi.astype(F32)).astype(BF16)


def wide(part):
    re, im = part[:, :B], part[:, B:]
    return jnp.concatenate([part, jnp.concatenate([-im, re], axis=1)], axis=0)


def weights(t):
    hi, lo = split(t)
    return wide(hi), wide(lo)


def dot(a, b):
    return jnp.dot(a, b, preferred_element_type=F32)


def mul(v, w):
    hi, lo = split(v)
    return (dot(lo, w[0]) + dot(hi, w[1])) + dot(hi, w[0])


def mulv(v, w):
    n = v.shape[0]
    hi, lo = split(v)
    both = jnp.concatenate([hi, lo], axis=0)
    a, b = dot(both, w[0]), dot(both, w[1])
    return (a[n:] + b[:n]) + a[:n]


def place(shift):
    d = lax.axis_index("depth")
    core = d & 1
    at = (d >> shift) & 3
    return jnp.where(core == 0, at, 3 - at)


def waves(direction, depth, lane):
    arg = WAVENUMBER * (jnp.sin(direction) * lane + jnp.cos(direction) * depth)
    return jnp.cos(arg), jnp.sin(arg)


def eights():
    row = lax.broadcasted_iota(jnp.int32, (FIELDS, B), 0)
    lane = lax.broadcasted_iota(jnp.int32, (FIELDS, B), 1).astype(F32)
    return row, lane, (row & 1) == 1


def prep_kernel(angles, choice, contrast, adj, blocks, own, oth, ang, pick, con, src, raw, sem):
    t = lax.axis_index("src")
    first = (lax.axis_index("depth") * 2).astype(F32)
    moves = ((blocks.at[:, t], raw), (choice, pick), (angles, ang), (contrast, con), (adj, src))
    copies = [pltpu.make_async_copy(f, g, sem.at[n]) for n, (f, g) in enumerate(moves)]
    for c in copies:
        c.start()
    row, lane, odd = eights()
    for c in copies[1:]:
        c.wait()
    turn = jnp.where(odd, jnp.full((FIELDS, B), ang[1]), jnp.full((FIELDS, B), ang[0])).astype(F32)
    is_f, is_a = row < 2, (row >= 4) & (row < 6)
    zero = jnp.zeros((FIELDS, B), F32)

    def tiled(line, tile):
        return jnp.where(tile == 0, line[:, :B], line[:, B:])

    for l in range(2):
        inc = waves(turn * (2.0 * math.pi / NANG), first + float(l), lane)
        own_con = jnp.broadcast_to(tiled(con[pl.ds(l, 1), :], t), (FIELDS, B))
        for p in range(2):
            part = slice(p * B, (p + 1) * B)
            lines = [src[p, i, pl.ds(l, 1), :] for i in range(2)]
            a = jnp.where(odd, tiled(lines[1], t), tiled(lines[0], t))
            own[l, B : B + 8, part] = jnp.where(is_f, inc[p] * own_con, jnp.where(is_a, a, zero))
            own[l, B + 8 : B + 16, part] = jnp.where(is_f, inc[p], zero)
            own[l, B + 16 : B + 24, part] = own_con
            for i in range(2):
                oth[2 * l + i : 2 * l + i + 1, part] = tiled(lines[i], 1 - t)
    for p in range(2):
        oth[4:8, p * B : (p + 1) * B] = jnp.full((4, B), ang[p]).astype(F32)
    copies[0].wait()
    for l in range(2):
        for p in range(2):
            own[l, :B, p * B : (p + 1) * B] = raw[pick[l], p].T


def chip_kernel(own, peer, x):
    core = lax.axis_index("depth") & 1
    g = [(own if s < 2 else peer)[(s & 1) ^ core, :B, :] for s in range(4)]
    x01 = mul(g[0], weights(g[1]))
    x23 = mul(g[2], weights(g[3]))
    x[...] = mul(x01, weights(x23))


def offset_kernel(own, peer, same, cross, c, hi):
    d = lax.axis_index("depth")
    core = d & 1
    row, lane, odd = eights()
    is_f, is_a = (row >= 2) & (row < 4), row >= 6
    zero = jnp.zeros((FIELDS, B), F32)
    v = jnp.zeros((FIELDS, W2), F32)
    for k in range(4):
        a, b = (own, same) if k < 2 else (peer, cross)
        l = k & 1
        depth = ((d >> 1) * 4 + ((k >> 1) ^ core) * 2 + l).astype(F32)
        turn = jnp.where(odd, b[4:5, B:], b[4:5, :B])
        inc = waves(turn * (2.0 * math.pi / NANG), depth, lane)
        con = a[l, B + 16 : B + 24, :B]
        h, n = [], []
        for p in range(2):
            part = slice(p * B, (p + 1) * B)
            line = jnp.where(odd, b[2 * l + 1 : 2 * l + 2, part], b[2 * l : 2 * l + 1, part])
            h.append(a[l, B : B + 8, part] + jnp.where(is_f, inc[p] * con, jnp.where(is_a, line, zero)))
            n.append(a[l, B + 8 : B + 16, part] + jnp.where(is_f, inc[p], zero))
        h = jnp.concatenate(h, axis=1)
        hi[k, :8, :] = h
        hi[k, 8:, :] = jnp.concatenate(n, axis=1)
        v = mulv(v + h, weights(a[l, :B, :]))
    c[...] = jnp.where(core == 0, v, 0.0)


def pair_kernel(shift, mine, theirs, x, second):
    late = (place(shift) & 1) == 1
    a = jnp.where(late, theirs[...], mine[...])
    b = jnp.where(late, mine[...], theirs[...])
    second[...] = b
    x[...] = mul(a, weights(b))


def pair_rows_kernel(shift, mine, theirs, second, c):
    late = (place(shift) & 1) == 1
    a = jnp.where(late, theirs[...], mine[...])
    b = jnp.where(late, mine[...], theirs[...])
    c[...] = mulv(a, weights(second[...])) + b


def quad_kernel(shift, mine, theirs, c_mine, c_theirs, mate, c_mate, x, p, second):
    q = place(shift)
    late, odd = q >= 2, (q & 1) == 1
    a = jnp.where(late, theirs[...], mine[...])
    b = jnp.where(late, mine[...], theirs[...])
    ca = jnp.where(late, c_theirs[...], c_mine[...])
    cb = jnp.where(late, c_mine[...], c_theirs[...])
    w = weights(b)
    x[:B, :] = mul(a, w)
    x[B:, :] = mulv(ca, w) + cb
    second[...] = b
    row = lax.broadcasted_iota(jnp.int32, (B, W2), 0)
    col = lax.broadcasted_iota(jnp.int32, (B, W2), 1)
    base = jnp.where(late, a, jnp.where(row == col, 1.0, 0.0))
    c_base = jnp.where(late, ca, 0.0)
    w = weights(mate[...])
    p[:B, :] = jnp.where(odd, mul(base, w), base)
    p[B:, :] = jnp.where(odd, mulv(c_base, w) + c_mate[...], c_base)


def quad_rows_kernel(shift, mine, theirs, second, mate, c_mate, total, part):
    q = place(shift)
    late, odd = q >= 2, (q & 1) == 1
    a = jnp.where(late, theirs[...], mine[...])
    b = jnp.where(late, mine[...], theirs[...])
    total[...] = mulv(a, weights(second[...])) + b
    base = jnp.where(late, a, 0.0)
    part[...] = jnp.where(odd, mulv(base, weights(mate[...])) + c_mate[...], base)


def level_kernel(shift, r0, r1, r2, r3, x, s, p, v):
    q = place(shift)
    for k, r in enumerate((r0, r1, r2, r3)):
        s[q ^ k] = r[...]
    row = lax.broadcasted_iota(jnp.int32, (ROWS, W2), 0)
    col = lax.broadcasted_iota(jnp.int32, (ROWS, W2), 1)
    tail = row >= B

    def step(a, b):
        return mul(a, weights(b[:B])) + jnp.where(tail, b, 0.0)

    s0, s1, s2, s3 = (s[k] for k in range(4))
    x01 = step(s0, s1)
    x23 = step(s2, s3)
    x[...] = step(x01, x23)
    x012 = step(x01, s2)
    one = jnp.where((row == col) & (row < B), 1.0, 0.0)
    p[...] = jnp.where(q == 0, one, jnp.where(q == 1, s0, jnp.where(q == 2, x01, x012)))
    v[0] = x23[:B]
    v[1] = mul(s1[:B], weights(x23[:B]))


def turn_kernel(r0, r1, r2, r3, pz, px, own, peer, hi, out, s):
    q = place(5)
    for k, r in enumerate((r0, r1, r2, r3)):
        s[q ^ k] = r[...]
    a = jnp.where(q > 0, s[0, B:, :], 0.0)
    for k in (1, 2):
        a = jnp.where(q > k, mulv(a, weights(s[k, :B, :])) + s[k, B:, :], a)
    for p in (px, pz):
        a = mulv(a, weights(p[:B, :])) + p[B:, :]
    ws, ds = [], []
    for k in range(4):
        w = weights((own if k < 2 else peer)[k & 1, :B, :])
        a = mulv(a + hi[k, :8, :], w)
        ws.append(w)
        ds.append(a)
        out[8 + 8 * k : 16 + 8 * k, :] = a
    u = ds[3]
    for k in (2, 1, 0):
        u = ds[k] + mulv(u, ws[k])
    out[:8, :] = u


def gather_kernel(shift, r0, r1, r2, r3, s, v, total, part, e):
    q = place(shift)
    for k, r in enumerate((r0, r1, r2, r3)):
        e[q ^ k] = r[...]
    total[...] = (
        (mulv(e[0], weights(v[1])) + mulv(e[1], weights(v[0])))
        + mulv(e[2], weights(s[3, :B, :]))
        + e[3]
    )
    c = jnp.where(q > 0, e[0], 0.0)
    for k in (1, 2):
        c = jnp.where(q > k, mulv(c, weights(s[k, :B, :])) + e[k], c)
    part[...] = c


def last_kernel(e0, e1, e2, e3, r0, r1, r2, r3, px, pz, cx, cz, own, peer, hi, d, grad, e, s):
    q = place(5)
    for k, (f, r) in enumerate(((e0, r0), (e1, r1), (e2, r2), (e3, r3))):
        e[q ^ k] = f[...]
        s[q ^ k] = r[...]
    u = jnp.where(q > 0, e[0], 0.0)
    for k in (1, 2):
        u = jnp.where(q > k, mulv(u, weights(s[k, :B, :])) + e[k], u)
    for p, c in ((px, cx), (pz, cz)):
        u = mulv(u, weights(p[:B, :])) + c[...]
    for k in (3, 2, 1, 0):
        g = peer if k < 2 else own
        u = d[8 + 8 * k : 16 + 8 * k, :] + mulv(u, weights(g[k & 1, :B, :]))
        f = u + hi[k ^ 2, 8:, :]
        prod = f[:4] * f[4:]
        tot = jnp.sum(prod, axis=0, keepdims=True)
        grad[k : k + 1, :] = (tot[:, :B] - tot[:, B:]) * 0.25


def call(kernel, outs, *args, scratch=(), in_specs=None):
    shapes = [jax.ShapeDtypeStruct(o, F32) for o in outs]
    vm = pl.BlockSpec(memory_space=pltpu.VMEM)
    got = pl.pallas_call(
        kernel,
        out_shape=shapes,
        in_specs=in_specs or [vm] * len(args),
        out_specs=[vm] * len(outs),
        scratch_shapes=list(scratch),
        compiler_params=pltpu.CompilerParams(vmem_limit_bytes=8 << 20),
        cost_estimate=pl.CostEstimate(flops=200_000_000, bytes_accessed=1_000_000, transcendentals=0),
    )(*args)
    return got[0] if len(outs) == 1 else got


def flip(value, bit, depth):
    return lax.ppermute(value, "depth", [(i, i ^ bit) for i in range(depth)])


def gather4(value, bit, depth):
    return [value] + [flip(value, k * bit, depth) for k in (1, 2, 3)]


def per_device(angles, factor_choice, contrast, adjoint_source, inverse_blocks):
    depth = lax.axis_size("depth")
    core = lax.axis_index("depth") & 1
    own, oth = call(
        prep_kernel,
        [(2, B + 24, W2), (8, W2)],
        *[pltpu.with_memory_space_constraint(v, pltpu.HBM)
          for v in (angles, factor_choice, contrast, adjoint_source, inverse_blocks)],
        in_specs=[pl.BlockSpec(memory_space=pltpu.HBM)] * 5,
        scratch=[
            pltpu.SMEM((2,), jnp.int32),
            pltpu.SMEM((2,), jnp.int32),
            pltpu.VMEM((2, W2), F32),
            pltpu.VMEM((2, 2, 2, W2), F32),
            pltpu.VMEM((2, 2, B, B), F32),
            pltpu.SemaphoreType.DMA((5,)),
        ],
    )
    peer = flip(own, 1, depth)
    xm = call(chip_kernel, [(B, W2)], own, peer)
    mate = flip(xm, 2, depth)
    same = lax.ppermute(oth, "src", [(0, 1), (1, 0)])
    across = [(2 * i + t, 2 * (i ^ 1) + (1 - t)) for i in range(depth) for t in range(2)]
    cross = lax.ppermute(oth, ("depth", "src"), across)
    x2, s1 = call(functools.partial(pair_kernel, 1), [(B, W2)] * 2, xm, mate)
    x2_far = flip(x2, 4, depth)
    rows = (FIELDS, W2)
    c, hi = call(offset_kernel, [rows, (4, 16, W2)], own, peer, same, cross)
    c_mate = flip(c, 2, depth)
    c2 = call(functools.partial(pair_rows_kernel, 1), [rows], c, c_mate, s1)
    c2_far = flip(c2, 4, depth)
    x, pz, s2 = call(
        functools.partial(quad_kernel, 1), [(ROWS, W2), (ROWS, W2), (B, W2)],
        x2, x2_far, c2, c2_far, mate, c_mate,
    )
    outs = [(ROWS, W2), (4, ROWS, W2), (ROWS, W2), (2, B, W2)]
    x, sx, px, vx = call(functools.partial(level_kernel, 3), outs, *gather4(x, 8, depth))
    ry = gather4(x, 32, depth)
    big = pltpu.VMEM((4, ROWS, W2), F32)
    small = pltpu.VMEM((4, FIELDS, W2), F32)
    sent = call(turn_kernel, [(40, W2)], *ry, pz, px, own, peer, hi, scratch=[big])
    d = flip(sent, 1, depth)
    e = d[:FIELDS]
    e_mate = flip(e, 2, depth)
    e2 = call(functools.partial(pair_rows_kernel, 1), [rows], e, e_mate, s1)
    e2_far = flip(e2, 4, depth)
    e, cz = call(functools.partial(quad_rows_kernel, 1), [rows, rows], e2, e2_far, s2, mate, e_mate)
    ex = gather4(e, 8, depth)
    e, cx = call(functools.partial(gather_kernel, 3), [rows, rows], *ex, sx, vx, scratch=[small])
    ey = gather4(e, 32, depth)
    grad = call(
        last_kernel, [(4, B)], *ey, *ry, px, pz, cx, cz, own, peer, hi, d,
        scratch=[small, big],
    )
    back = flip(grad[:2], 1, depth)
    return jnp.where(core == 0, back, grad[2:])


def solution(mesh):
    placed = (
        P("src"),
        P("depth"),
        P("depth", None),
        P(None, "src", "depth", None),
        P("depth", None, None, None, None),
    )
    return jax.shard_map(
        per_device, mesh=mesh, in_specs=placed, out_specs=P("depth", "src"), check_vma=False
    )
```
